512 devices in a mesh: tgt: 16 (over y, core), src: 32 (over z, x).
Axes of the slice: x: 4, y: 8, z: 8, core: 2. Of those that a mesh axis runs over, the one named last changes fastest.
Arguments:
- trial_vectors: float32 [8, 512, 128], P(None, ('tgt', 'src')), may hold values from -18 to 18
- couplings: float32 [512, 32, 128, 128], P('tgt', 'src'), may hold values from -0.125 to 0.125
- neighbours: int32 [512, 32], P('tgt', 'src'), may hold values from 0 to 511, as said below
- live_slots: int32 [512, 32], P('tgt', 'src'), may hold values from 0 to 1, as said below
- energies: float32 [512, 128], P(('tgt', 'src')), may hold values from 1 to 3
Outputs:
- sigma_vectors: float32 [8, 512, 128], P(None, ('tgt', 'src'))
- residual: float32 [8, 512, 128], P(None, ('tgt', 'src'))
- residual_norms: float32 [8], replicated
The draws below stay inside these ranges and needn't reach their ends.
Inputs may be any that keep to these rules, and one draw needn't show every extreme that they name: `neighbours`: each entry differs from its own chromophore's index by at most 16. `live_slots`: some chromophore has all 32 slots live.
All inputs are finite; a program needn't handle non-finite values.
Results may differ from the reference program's by a relative error of at most 0.000062.
Values sent between devices are 32-bit elements; how exact they have to be, the bound alone decides.
A program may use at most 64 MiB of HBM per device.

```python
import jax
import jax.numpy as jnp
from jax import lax

S = 128
K = 8
NB = 32
M = 512
REACH = 16
N_TGT = 16


def neighbour_table(key):
    inner_key = jax.random.fold_in(key, 7)
    keys_rows = jax.random.split(inner_key, M)
    orders = jax.vmap(lambda subkey: jax.random.permutation(subkey, 2 * REACH))(keys_rows)[:, :NB]
    offsets = jnp.where(orders < REACH, orders - REACH, orders - REACH + 1).astype(jnp.int32)
    row_index = jnp.arange(M, dtype=jnp.int32)[:, None]
    target = row_index + offsets
    inside = (target >= 0) & (target < M)
    counts = jax.random.randint(jax.random.fold_in(key, 11), (M, 1), NB // 2, NB + 1)
    full_row = jax.random.randint(jax.random.fold_in(key, 13), (), REACH, M - REACH)
    counts = jnp.where(row_index == full_row, NB, counts)
    slot_index = jnp.arange(NB, dtype=jnp.int32)[None, :]
    live = ((slot_index < counts) & inside).astype(jnp.int32)
    chosen = jnp.where(inside, target, row_index).astype(jnp.int32)
    return (chosen, live)


def draw_neighbours(key, part):
    return neighbour_table(key)[0]


def draw_live_slots(key, part):
    return neighbour_table(key)[1]


def draw_trial_vectors(key, part):
    first_key = jax.random.fold_in(key, 21)
    position = jnp.arange(M, dtype=jnp.float32) / M
    rising = (3.0 ** position)[None, :, None]
    values = jax.random.normal(first_key, (K, M, S), jnp.float32) * rising
    return jnp.clip(values, -18.0, 18.0).astype(jnp.float32)


def levels(own_key, shape, cuts, low, top_value):
    def one(dim, parts):
        steps = jax.random.uniform(jax.random.fold_in(jax.random.fold_in(own_key, 6), dim), (parts,), jnp.float32, low / len(cuts), top_value / len(cuts))
        return jnp.repeat(jnp.exp(steps), shape[dim] // parts).reshape((-1,) + (1,) * (len(shape) - dim - 1))

    level = one(*cuts[0])
    for cut in cuts[1:]:
        level = level * one(*cut)
    return level


def centred(own_key, shape, spread, reach, shards=(), kind=jnp.bfloat16):
    loudness = levels(own_key, shape, shards, -0.22, 0.18) if shards else 1.0
    values = jax.random.normal(own_key, shape, jnp.float32) * spread * loudness
    return jnp.minimum(jnp.maximum(values, -reach), reach).astype(kind)


def setup_inputs(seed: int = 0) -> dict:
    splits = jax.random.split(jax.random.key(seed), 6)
    trial_vectors = draw_trial_vectors(jax.random.fold_in(splits[5], 71), 0)
    couplings = centred(splits[1], (M, NB, S, S), (S * NB // 2) ** -0.5, 0.125, ((0, 16), (1, 32)), jnp.float32)
    neighbours = draw_neighbours(jax.random.fold_in(splits[5], 71), 0)
    live_slots = draw_live_slots(jax.random.fold_in(splits[5], 71), 0)
    energies = jnp.clip(1.0 + 2.0 * jax.random.uniform(splits[4], (M, S), jnp.float32) ** levels(splits[4], (M, S), ((0, 512),), -0.2, 0.2), 1.0, 3.0)
    return dict(trial_vectors=trial_vectors, couplings=couplings, neighbours=neighbours, live_slots=live_slots, energies=energies)


def reference(trial_vectors, couplings, neighbours, live_slots, energies):
    vectors, chromos, states = trial_vectors.shape
    slot_weight = live_slots.astype(jnp.float32)

    def one_block(pieces):
        tiles, index_rows, weight_rows = pieces
        fetched = jnp.take(trial_vectors, index_rows.reshape(-1), axis=1)
        fetched = fetched.reshape(vectors, index_rows.shape[0], index_rows.shape[1], states)
        fetched = fetched * weight_rows[None, :, :, None]
        return jnp.einsum('inab,kinb->kia', tiles, fetched, precision=lax.Precision.HIGHEST)
    stacked = lax.map(one_block, (couplings.reshape(N_TGT, -1, NB, states, states), neighbours.reshape(N_TGT, -1, NB), slot_weight.reshape(N_TGT, -1, NB)))
    coupled = jnp.transpose(stacked, (1, 0, 2, 3)).reshape(vectors, chromos, states)
    sigmas = coupled + energies[None] * trial_vectors
    projected = jnp.einsum('kia,lia->kl', trial_vectors, sigmas, precision=lax.Precision.HIGHEST)
    metric = jnp.einsum('kia,lia->kl', trial_vectors, trial_vectors, precision=lax.Precision.HIGHEST)
    factor = jnp.linalg.cholesky(metric)
    mixing = jax.scipy.linalg.cho_solve((factor, True), projected)
    residual = sigmas - jnp.einsum('kia,kl->lia', trial_vectors, mixing, precision=lax.Precision.HIGHEST)
    totals = lax.optimization_barrier(jnp.sum(residual * residual, axis=(1, 2)))
    residual_norms = jnp.sqrt(totals / jnp.diagonal(metric))
    return (sigmas, residual, residual_norms)
```

```python
import functools

import jax
import jax.numpy as jnp
from jax import lax
from jax.experimental import pallas as pl
from jax.experimental.pallas import tpu as pltpu
from jax.sharding import PartitionSpec as P

MESH = pl.DeviceIdType.MESH
F32 = jnp.float32
BF16 = jnp.bfloat16
HIGHEST = lax.Precision.HIGHEST

NZ, NX, NT = 8, 4, 16
NS = NZ * NX
K, S = 8, 128
CHUNK = 8
NT_DIMS = (((1,), (1,)), ((), ()))


def remote(src, dst, send_sem, recv_sem, device):
    return pltpu.make_async_remote_copy(
        src_ref=src,
        dst_ref=dst,
        send_sem=send_sem,
        recv_sem=recv_sem,
        device_id=device,
        device_id_type=MESH,
    )


def drain(ref, sem):
    pltpu.make_async_copy(ref, ref, sem).wait()


def as_row(pairs):
    full = jnp.concatenate([pairs, jnp.zeros_like(pairs)], axis=0)
    return lax.dot_general(
        jnp.ones((8, S), F32), full, NT_DIMS, precision=HIGHEST, preferred_element_type=F32
    )


def as_tile(row):
    return pltpu.roll(jnp.broadcast_to(row, (K, S)), S - K * (K - 1), 1, stride=K, stride_axis=0)


def kernel(
    trial_hbm,
    couplings_hbm,
    neighbours_hbm,
    live_hbm,
    energies_hbm,
    sigma_ref,
    residual_ref,
    norms_ref,
    own,
    energy,
    raw,
    halves,
    index,
    live,
    rows,
    parts,
    sums,
    row_p,
    row_g,
    row_q,
    row_r,
    row_s,
    tgt_p,
    plane_p,
    tgt_g,
    plane_r,
    tgt_r,
    load_sem,
    chunk_sem,
    z_send,
    z_recv,
    x_send,
    x_recv,
    part_send,
    part_recv,
    small_send,
    small_recv,
):
    t, s = lax.axis_index("tgt"), lax.axis_index("src")
    z, x = s // NX, s % NX

    loads = [
        pltpu.make_async_copy(trial_hbm, own, load_sem.at[0]),
        pltpu.make_async_copy(energies_hbm, energy, load_sem.at[1]),
        pltpu.make_async_copy(neighbours_hbm, index, load_sem.at[2]),
        pltpu.make_async_copy(live_hbm, live, load_sem.at[3]),
    ]
    for load in loads:
        load.start()
    fetches = [
        pltpu.make_async_copy(
            couplings_hbm.at[pl.ds(c * CHUNK, CHUNK)], raw.at[pl.ds(c * CHUNK, CHUNK)], chunk_sem.at[c]
        )
        for c in range(NS // CHUNK)
    ]
    for fetch in fetches:
        fetch.start()

    barrier = pltpu.get_barrier_semaphore()

    def greet(device):
        pl.semaphore_signal(barrier, inc=1, device_id=device, device_id_type=MESH)

    def greet_z(d, _):
        greet((t, ((z + d) % NZ) * NX + x))

    def greet_x(d, _):
        greet((t, z * NX + (x + d) % NX))

    def greet_t(d, _):
        greet(((t + d) % NT, s))

    def greet_halo(j, _):
        greet(((t + 1 + (NT - 2) * (j // 4)) % NT, j * NX + x))

    lax.fori_loop(0, NZ, greet_halo, None)
    lax.fori_loop(1, NZ, greet_z, None)
    lax.fori_loop(1, NT, greet_t, None)
    lax.fori_loop(1, NX, greet_x, None)

    def split(i, _):
        tile = raw[i]
        high = tile.astype(BF16)
        halves[i, :, 0:S] = high
        halves[i, :, S : 2 * S] = (tile - high.astype(F32)).astype(BF16)

    for c, fetch in enumerate(fetches):
        fetch.wait()
        lax.fori_loop(c * CHUNK, (c + 1) * CHUNK, split, None, unroll=2)

    for load in loads:
        load.wait()
    pl.semaphore_wait(barrier, 2 * NZ - 1 + NX - 1 + NT - 1)

    block, other = (t % 2) * NS, (1 - t % 2) * NS
    mine = block + s
    next_t = (t + NT - 1 + 2 * (z // 4)) % NT

    def send_z(d, _):
        to = ((z + d) % NZ) * NX + x
        remote(own, rows.at[mine], z_send.at[0], z_recv.at[z], (t, to)).start()

    def send_halo(d, _):
        to = ((z + d) % NZ) * NX + x
        remote(own, rows.at[mine], z_send.at[0], z_recv.at[NZ + z], (next_t, to)).start()

    def forward(src, at):
        def send_x(d, _):
            to = z * NX + (x + d) % NX
            remote(src, rows.at[at], x_send.at[0], x_recv.at[0], (t, to)).start()

        lax.fori_loop(1, NX, send_x, None)

    lax.fori_loop(0, NZ, send_halo, None)
    lax.fori_loop(1, NZ, send_z, None)
    here = pltpu.make_async_copy(own, rows.at[mine], load_sem.at[0])
    here.start()
    forward(own, mine)
    for d in (1, 7, 2, 6, 3, 5, 4):
        j = (z + d) % NZ
        at = block + j * NX + x
        drain(rows.at[at], z_recv.at[j])
        forward(rows.at[at], at)
    for d in (0, 1, 7, 2, 6, 3, 5, 4):
        j = (z + d) % NZ
        at = other + j * NX + x
        drain(rows.at[at], z_recv.at[NZ + j])
        forward(rows.at[at], at)
    here.wait()
    drain(rows.at[pl.ds(0, 48)], x_recv.at[0])

    def share(i, pairs):
        found = rows[index[0, i] % 64] * live[0, i].astype(F32)
        high = found.astype(BF16).astype(F32)
        low = found - high
        left = jnp.concatenate(
            [jnp.concatenate([high, low], 0), jnp.concatenate([high, jnp.zeros_like(high)], 0)], 1
        ).astype(BF16)
        both = lax.dot_general(left, halves[i], NT_DIMS, preferred_element_type=F32)
        part = both[0:K] + both[K : 2 * K]
        parts[i] = part
        vector = rows[block + i]
        return tuple(
            pairs[l] + vector * jnp.broadcast_to(part[l : l + 1], (K, S)) for l in range(K)
        )

    zeros = tuple(jnp.zeros((K, S), F32) for _ in range(K))
    pairs = lax.fori_loop(0, NS, share, zeros, unroll=8)
    vector = own[...]
    diagonal = vector * energy[...]
    pairs = [
        pairs[l] + vector * jnp.broadcast_to(diagonal[l : l + 1], (K, S)) for l in range(K)
    ]
    row_p[...] = as_row(jnp.concatenate(pairs[::-1], 0))

    def send_tgt(src, buf, sem):
        def one(d, _):
            remote(
                src.at[pl.ds(0, 1)],
                buf.at[pl.ds(t, 1)],
                small_send.at[sem],
                small_recv.at[sem],
                ((t + d) % NT, s),
            ).start()

        lax.fori_loop(1, NT, one, None)
        buf[pl.ds(t, 1), :] = src[0:1, :]

    def wait_tgt(buf, sem):
        drain(buf.at[pl.ds(0, NT - 1)], small_recv.at[sem])
        return jnp.sum(buf[...], axis=0, keepdims=True)

    def send_plane(src, buf, sem):
        def one(d, _):
            to = ((z + d // NX) % NZ) * NX + (x + d % NX) % NX
            remote(
                src.at[pl.ds(0, 1)],
                buf.at[pl.ds(s, 1)],
                small_send.at[sem],
                small_recv.at[sem],
                (t, to),
            ).start()

        lax.fori_loop(1, NS, one, None)
        buf[pl.ds(s, 1), :] = src[0:1, :]

    def wait_plane(buf, sem):
        drain(buf.at[pl.ds(0, NS - 1)], small_recv.at[sem])
        return jnp.sum(buf[...], axis=0, keepdims=True)

    send_tgt(row_p, tgt_p, 0)

    def send_part(d, _):
        to = ((z + d // NX) % NZ) * NX + (x + d % NX) % NX
        remote(parts.at[to], sums.at[s], part_send.at[0], part_recv.at[0], (t, to)).start()

    lax.fori_loop(1, NS, send_part, None)

    def gram(i, pairs):
        vector = rows[block + i]
        return tuple(
            pairs[l] + vector * jnp.broadcast_to(vector[l : l + 1], (K, S)) for l in range(K)
        )

    pairs = lax.fori_loop(0, NS, gram, zeros, unroll=8)
    row_g[...] = as_row(jnp.concatenate(pairs[::-1], 0))
    send_tgt(row_g, tgt_g, 1)

    row_q[...] = jnp.broadcast_to(wait_tgt(tgt_p, 0), (8, S))
    send_plane(row_q, plane_p, 2)

    metric = as_tile(wait_tgt(tgt_g, 1))
    lane = lax.broadcasted_iota(jnp.int32, (K, S), 1)
    sub = lax.broadcasted_iota(jnp.int32, (K, S), 0)
    norms2 = jnp.sum(jnp.where(lane == sub, metric, 0.0), axis=0, keepdims=True)
    work = metric
    solved = vector
    factors = []
    for j in range(K):
        column = jnp.broadcast_to(work[:, j : j + 1], (K, S))
        pivot = lax.rsqrt(jnp.broadcast_to(column[j : j + 1], (K, S)))
        column = jnp.where(sub >= j, column * pivot, 0.0)
        factors.append((column, pivot))
        line = jnp.sum(jnp.where(lane == sub, column, 0.0), axis=0, keepdims=True)
        work = work - column * jnp.broadcast_to(line, (K, S))
        top = jnp.broadcast_to(solved[j : j + 1], (K, S)) * pivot
        solved = jnp.where(sub == j, top, solved - jnp.where(sub > j, column * top, 0.0))
    for j in reversed(range(K)):
        column, pivot = factors[j]
        dots = jnp.sum(jnp.where(sub > j, column * solved, 0.0), axis=0, keepdims=True)
        value = (solved - jnp.broadcast_to(dots, (K, S))) * pivot
        solved = jnp.where(sub == j, value, solved)

    drain(sums.at[pl.ds(0, NS - 1)], part_recv.at[0])
    sums[s] = parts[s]
    sigma = jnp.sum(sums[...], axis=0) + diagonal
    sigma_ref[...] = sigma

    projected = as_tile(wait_plane(plane_p, 2))
    residual = sigma
    for j in range(K):
        residual = residual - jnp.broadcast_to(projected[:, j : j + 1], (K, S)) * jnp.broadcast_to(
            solved[j : j + 1], (K, S)
        )
    residual_ref[...] = residual
    square = residual * residual
    row_r[...] = lax.dot_general(
        jnp.ones((8, S), F32),
        jnp.concatenate([square, jnp.zeros((S - K, S), F32)], 0),
        NT_DIMS,
        precision=HIGHEST,
        preferred_element_type=F32,
    )
    send_plane(row_r, plane_r, 3)
    row_s[...] = jnp.broadcast_to(wait_plane(plane_r, 3), (8, S))
    send_tgt(row_s, tgt_r, 4)
    total = wait_tgt(tgt_r, 4)
    norms_ref[...] = jnp.sqrt(total / jnp.where(lane[0:1] < K, norms2, 1.0))

    drain(rows.at[pl.ds(0, 2 * NZ - 1)], z_send.at[0])
    drain(rows.at[pl.ds(0, 48)], x_send.at[0])
    drain(parts.at[pl.ds(0, NS - 1)], part_send.at[0])
    for sem, buf, count in ((0, tgt_p, NT), (1, tgt_g, NT), (2, plane_p, NS), (3, plane_r, NS), (4, tgt_r, NT)):
        drain(buf.at[pl.ds(0, count - 1)], small_send.at[sem])


def shards(trial_vectors, couplings, neighbours, live_slots, energies):
    hbm = pl.BlockSpec(memory_space=pltpu.HBM)
    vmem = pl.BlockSpec(memory_space=pltpu.VMEM)
    dma = pltpu.SemaphoreType.DMA
    sigma, residual, norms = pl.pallas_call(
        kernel,
        out_shape=(
            jax.ShapeDtypeStruct((K, S), F32),
            jax.ShapeDtypeStruct((K, S), F32),
            jax.ShapeDtypeStruct((1, S), F32),
        ),
        in_specs=[hbm] * 5,
        out_specs=(vmem, vmem, vmem),
        scratch_shapes=[
            pltpu.VMEM((K, S), F32),
            pltpu.VMEM((1, S), F32),
            pltpu.VMEM((NS, S, S), F32),
            pltpu.VMEM((NS, S, 2 * S), BF16),
            pltpu.SMEM((1, NS), jnp.int32),
            pltpu.SMEM((1, NS), jnp.int32),
            pltpu.VMEM((64, K, S), F32),
            pltpu.VMEM((NS, K, S), F32),
            pltpu.VMEM((NS, K, S), F32),
            pltpu.VMEM((8, S), F32),
            pltpu.VMEM((8, S), F32),
            pltpu.VMEM((8, S), F32),
            pltpu.VMEM((8, S), F32),
            pltpu.VMEM((8, S), F32),
            pltpu.VMEM((NT, S), F32),
            pltpu.VMEM((NS, S), F32),
            pltpu.VMEM((NT, S), F32),
            pltpu.VMEM((NS, S), F32),
            pltpu.VMEM((NT, S), F32),
            dma((4,)),
            dma((NS // CHUNK,)),
            dma((1,)),
            dma((2 * NZ,)),
            dma((1,)),
            dma((1,)),
            dma((1,)),
            dma((1,)),
            dma((5,)),
            dma((5,)),
        ],
        compiler_params=pltpu.CompilerParams(collective_id=0, has_side_effects=True),
        name="davidson",
    )(
        trial_vectors.reshape(K, S),
        couplings.reshape(NS, S, S),
        neighbours.reshape(1, NS),
        live_slots.reshape(1, NS),
        energies,
    )
    return sigma.reshape(K, 1, S), residual.reshape(K, 1, S), norms[0, :K]


def solution(mesh):
    return jax.shard_map(
        shards,
        mesh=mesh,
        in_specs=(
            P(None, ("tgt", "src"), None),
            P("tgt", "src", None, None),
            P("tgt", "src"),
            P("tgt", "src"),
            P(("tgt", "src"), None),
        ),
        out_specs=(P(None, ("tgt", "src"), None), P(None, ("tgt", "src"), None), P()),
        check_vma=False,
    )
```

```python
import functools

import jax
import jax.numpy as jnp
from jax import lax
from jax.experimental import pallas as pl
from jax.experimental.pallas import tpu as pltpu
from jax.sharding import PartitionSpec as P

MESH = pl.DeviceIdType.MESH
F32 = jnp.float32
BF16 = jnp.bfloat16
HIGHEST = lax.Precision.HIGHEST

NZ, NX, NT = 8, 4, 16
NS = NZ * NX
K, S = 8, 128
CHUNK = 8
NT_DIMS = (((1,), (1,)), ((), ()))


def remote(src, dst, send_sem, recv_sem, device):
    return pltpu.make_async_remote_copy(
        src_ref=src,
        dst_ref=dst,
        send_sem=send_sem,
        recv_sem=recv_sem,
        device_id=device,
        device_id_type=MESH,
    )


def drain(ref, sem):
    pltpu.make_async_copy(ref, ref, sem).wait()


def as_row(pairs):
    full = jnp.concatenate([pairs, jnp.zeros_like(pairs)], axis=0)
    return lax.dot_general(
        jnp.ones((8, S), F32), full, NT_DIMS, precision=HIGHEST, preferred_element_type=F32
    )


def as_tile(row):
    return pltpu.roll(jnp.broadcast_to(row, (K, S)), S - K * (K - 1), 1, stride=K, stride_axis=0)


def kernel(
    trial_hbm,
    couplings_hbm,
    neighbours_hbm,
    live_hbm,
    energies_hbm,
    packed_ref,
    own,
    energy,
    raw,
    halves,
    index,
    live,
    rows,
    parts,
    sums,
    row_p,
    row_g,
    row_q,
    row_r,
    row_s,
    tgt_p,
    plane_p,
    tgt_g,
    plane_r,
    tgt_r,
    load_sem,
    chunk_sem,
    in_z,
    in_x,
    in_t,
    up_send,
    up_recv,
    halo_recv,
    x_send,
    x_recv,
    bulk_send,
    bulk_recv,
    part_send,
    part_recv,
    small_send,
    small_recv,
):
    t, s = lax.axis_index("tgt"), lax.axis_index("src")
    z, x = s // NX, s % NX

    loads = [
        pltpu.make_async_copy(trial_hbm, own, load_sem.at[0]),
        pltpu.make_async_copy(energies_hbm, energy, load_sem.at[1]),
        pltpu.make_async_copy(neighbours_hbm, index, load_sem.at[2]),
        pltpu.make_async_copy(live_hbm, live, load_sem.at[3]),
    ]
    for load in loads:
        load.start()
    fetches = [
        pltpu.make_async_copy(
            couplings_hbm.at[pl.ds(c * CHUNK, CHUNK)], raw.at[pl.ds(c * CHUNK, CHUNK)], chunk_sem.at[c]
        )
        for c in range(NS // CHUNK)
    ]
    for fetch in fetches:
        fetch.start()

    barrier = pltpu.get_barrier_semaphore()
    halo_t = (t + NT - 1 + 2 * (z // 4)) % NT

    def signal(sem, device):
        pl.semaphore_signal(sem, inc=1, device_id=device, device_id_type=MESH)

    def greet_z(j, _):
        signal(barrier, (t, j * NX + x))
        signal(barrier, ((t + 1 + (NT - 2) * (j // 4)) % NT, j * NX + x))

    lax.fori_loop(z + 1, NZ, greet_z, None)
    lax.fori_loop(x + 1, NX, lambda j, _: signal(barrier, (t, z * NX + j)), None)
    lax.fori_loop(t + 1, NT, lambda j, _: signal(barrier, (j, s)), None)
    before = 2 * z + x + t

    @pl.when(before > 0)
    def _():
        pl.semaphore_wait(barrier, before)

    lax.fori_loop(0, z, lambda j, _: signal(in_z.at[z], (t, j * NX + x)), None)
    lax.fori_loop(0, x, lambda j, _: signal(in_x.at[x], (t, z * NX + j)), None)
    lax.fori_loop(0, t, lambda j, _: signal(in_t.at[t], (j, s)), None)

    block, other = (t % 2) * NS, (1 - t % 2) * NS
    mine = block + s

    loads[0].wait()

    def send_up(j, _):
        to = j * NX + x
        remote(own, rows.at[mine], up_send.at[j], halo_recv.at[z], (halo_t, to)).start()
        remote(own, rows.at[mine], up_send.at[j], up_recv.at[z], (t, to)).start()

    lax.fori_loop(0, z, send_up, None)
    here = pltpu.make_async_copy(own, rows.at[mine], load_sem.at[0])
    here.start()

    @pl.when(halo_t > t)
    def _():
        pl.semaphore_wait(in_t.at[halo_t], 1)

    remote(own, rows.at[mine], up_send.at[z], halo_recv.at[z], (halo_t, s)).start()

    def forward(src, at, j):
        def send_x(d, _):
            to = z * NX + (x + d) % NX
            remote(src, rows.at[at], x_send.at[j], x_recv.at[j], (t, to)).start()

        lax.fori_loop(1, NX, send_x, None)

    lax.fori_loop(x + 1, NX, lambda j, _: pl.semaphore_wait(in_x.at[j], 1), None)
    forward(own, mine, z)
    beside = other + s
    drain(rows.at[beside], halo_recv.at[z])
    forward(rows.at[beside], beside, z)

    def split(i, _):
        tile = raw[i]
        high = tile.astype(BF16)
        halves[i, :, 0:S] = high
        halves[i, :, S : 2 * S] = (tile - high.astype(F32)).astype(BF16)

    for c, fetch in enumerate(fetches):
        fetch.wait()
        lax.fori_loop(c * CHUNK, (c + 1) * CHUNK, split, None, unroll=2)
    for load in loads[1:]:
        load.wait()
    here.wait()
    drain(rows.at[pl.ds(0, 6)], x_recv.at[z])

    def after(j, _):
        pl.semaphore_wait(in_z.at[j], 1)
        for side in (block, other):
            four = rows.at[pl.ds(side + z * NX, NX)]
            remote(four, four, bulk_send.at[j], bulk_recv.at[z], (t, j * NX + x)).start()
        at = block + j * NX + x
        drain(rows.at[at], up_recv.at[j])
        forward(rows.at[at], at, j)
        at = other + j * NX + x
        drain(rows.at[at], halo_recv.at[j])
        forward(rows.at[at], at, j)

    lax.fori_loop(z + 1, NZ, after, None)
    lax.fori_loop(0, z, lambda j, _: drain(rows.at[pl.ds(0, 2 * NX)], bulk_recv.at[j]), None)
    lax.fori_loop(z + 1, NZ, lambda j, _: drain(rows.at[pl.ds(0, 6)], x_recv.at[j]), None)

    def share(i, pairs):
        found = rows[index[0, i] % 64] * live[0, i].astype(F32)
        high = found.astype(BF16).astype(F32)
        low = found - high
        left = jnp.concatenate(
            [jnp.concatenate([high, low], 0), jnp.concatenate([high, jnp.zeros_like(high)], 0)], 1
        ).astype(BF16)
        both = lax.dot_general(left, halves[i], NT_DIMS, preferred_element_type=F32)
        part = both[0:K] + both[K : 2 * K]
        parts[i] = part
        vector = rows[block + i]
        return tuple(
            pairs[l] + vector * jnp.broadcast_to(part[l : l + 1], (K, S)) for l in range(K)
        )

    zeros = tuple(jnp.zeros((K, S), F32) for _ in range(K))
    pairs = lax.fori_loop(0, NS, share, zeros, unroll=8)
    vector = own[...]
    diagonal = vector * energy[...]
    pairs = [
        pairs[l] + vector * jnp.broadcast_to(diagonal[l : l + 1], (K, S)) for l in range(K)
    ]
    row_p[...] = as_row(jnp.concatenate(pairs[::-1], 0))

    def send_tgt(src, buf, sem):
        def one(d, _):
            remote(
                src.at[pl.ds(0, 1)],
                buf.at[pl.ds(t, 1)],
                small_send.at[sem],
                small_recv.at[sem],
                ((t + d) % NT, s),
            ).start()

        lax.fori_loop(1, NT, one, None)
        buf[pl.ds(t, 1), :] = src[0:1, :]

    def wait_tgt(buf, sem):
        drain(buf.at[pl.ds(0, NT - 1)], small_recv.at[sem])
        return jnp.sum(buf[...], axis=0, keepdims=True)

    def send_plane(src, buf, sem):
        def one(d, _):
            to = ((z + d // NX) % NZ) * NX + (x + d % NX) % NX
            remote(
                src.at[pl.ds(0, 1)],
                buf.at[pl.ds(s, 1)],
                small_send.at[sem],
                small_recv.at[sem],
                (t, to),
            ).start()

        lax.fori_loop(1, NS, one, None)
        buf[pl.ds(s, 1), :] = src[0:1, :]

    def wait_plane(buf, sem):
        drain(buf.at[pl.ds(0, NS - 1)], small_recv.at[sem])
        return jnp.sum(buf[...], axis=0, keepdims=True)

    def wait_in(j, _):
        @pl.when(j != halo_t)
        def _():
            pl.semaphore_wait(in_t.at[j], 1)

    lax.fori_loop(t + 1, NT, wait_in, None)
    send_tgt(row_p, tgt_p, 0)

    def send_part(d, _):
        to = ((z + d // NX) % NZ) * NX + (x + d % NX) % NX
        remote(parts.at[to], sums.at[s], part_send.at[0], part_recv.at[0], (t, to)).start()

    lax.fori_loop(1, NS, send_part, None)

    def gram(i, pairs):
        vector = rows[block + i]
        return tuple(
            pairs[l] + vector * jnp.broadcast_to(vector[l : l + 1], (K, S)) for l in range(K)
        )

    pairs = lax.fori_loop(0, NS, gram, zeros, unroll=8)
    row_g[...] = as_row(jnp.concatenate(pairs[::-1], 0))
    send_tgt(row_g, tgt_g, 1)

    row_q[...] = jnp.broadcast_to(wait_tgt(tgt_p, 0), (8, S))
    send_plane(row_q, plane_p, 2)

    metric = as_tile(wait_tgt(tgt_g, 1))
    lane = lax.broadcasted_iota(jnp.int32, (K, S), 1)
    sub = lax.broadcasted_iota(jnp.int32, (K, S), 0)
    norms2 = jnp.sum(jnp.where(lane == sub, metric, 0.0), axis=0, keepdims=True)
    work = metric
    solved = vector
    factors = []
    for j in range(K):
        column = jnp.broadcast_to(work[:, j : j + 1], (K, S))
        pivot = lax.rsqrt(jnp.broadcast_to(column[j : j + 1], (K, S)))
        column = jnp.where(sub >= j, column * pivot, 0.0)
        factors.append((column, pivot))
        line = jnp.sum(jnp.where(lane == sub, column, 0.0), axis=0, keepdims=True)
        work = work - column * jnp.broadcast_to(line, (K, S))
        top = jnp.broadcast_to(solved[j : j + 1], (K, S)) * pivot
        solved = jnp.where(sub == j, top, solved - jnp.where(sub > j, column * top, 0.0))
    for j in reversed(range(K)):
        column, pivot = factors[j]
        dots = jnp.sum(jnp.where(sub > j, column * solved, 0.0), axis=0, keepdims=True)
        value = (solved - jnp.broadcast_to(dots, (K, S))) * pivot
        solved = jnp.where(sub == j, value, solved)

    drain(sums.at[pl.ds(0, NS - 1)], part_recv.at[0])
    sums[s] = parts[s]
    sigma = jnp.sum(sums[...], axis=0) + diagonal
    packed_ref[2 * K : 3 * K] = jnp.zeros((K, S), F32)
    packed_ref[0:K] = sigma

    projected = as_tile(wait_plane(plane_p, 2))
    residual = sigma
    for j in range(K):
        residual = residual - jnp.broadcast_to(projected[:, j : j + 1], (K, S)) * jnp.broadcast_to(
            solved[j : j + 1], (K, S)
        )
    packed_ref[K : 2 * K] = residual
    square = residual * residual
    row_r[...] = lax.dot_general(
        jnp.ones((8, S), F32),
        jnp.concatenate([square, jnp.zeros((S - K, S), F32)], 0),
        NT_DIMS,
        precision=HIGHEST,
        preferred_element_type=F32,
    )
    send_plane(row_r, plane_r, 3)
    row_s[...] = jnp.broadcast_to(wait_plane(plane_r, 3), (8, S))
    send_tgt(row_s, tgt_r, 4)
    total = wait_tgt(tgt_r, 4)
    packed_ref[2 * K : 2 * K + 1] = jnp.sqrt(total / jnp.where(lane[0:1] < K, norms2, 1.0))

    lax.fori_loop(0, z, lambda j, _: drain(rows.at[pl.ds(0, 2)], up_send.at[j]), None)
    drain(rows.at[0], up_send.at[z])
    lax.fori_loop(z, NZ, lambda j, _: drain(rows.at[pl.ds(0, 6)], x_send.at[j]), None)
    lax.fori_loop(
        z + 1, NZ, lambda j, _: drain(rows.at[pl.ds(0, 2 * NX)], bulk_send.at[j]), None
    )
    drain(parts.at[pl.ds(0, NS - 1)], part_send.at[0])
    for sem, buf, count in ((0, tgt_p, NT), (1, tgt_g, NT), (2, plane_p, NS), (3, plane_r, NS), (4, tgt_r, NT)):
        drain(buf.at[pl.ds(0, count - 1)], small_send.at[sem])


def finish(packed_ref, sigma_ref, residual_ref, norms_ref):
    sigma_ref[...] = packed_ref[0:K]
    residual_ref[...] = packed_ref[K : 2 * K]
    norms_ref[...] = packed_ref[2 * K : 2 * K + 1, 0:K]


def shards(trial_vectors, couplings, neighbours, live_slots, energies):
    hbm = pl.BlockSpec(memory_space=pltpu.HBM)
    vmem = pl.BlockSpec(memory_space=pltpu.VMEM)
    dma = pltpu.SemaphoreType.DMA
    regular = pltpu.SemaphoreType.REGULAR
    packed = pl.pallas_call(
        kernel,
        out_shape=jax.ShapeDtypeStruct((3 * K, S), F32),
        in_specs=[hbm] * 5,
        out_specs=vmem,
        scratch_shapes=[
            pltpu.VMEM((K, S), F32),
            pltpu.VMEM((1, S), F32),
            pltpu.VMEM((NS, S, S), F32),
            pltpu.VMEM((NS, S, 2 * S), BF16),
            pltpu.SMEM((1, NS), jnp.int32),
            pltpu.SMEM((1, NS), jnp.int32),
            pltpu.VMEM((64, K, S), F32),
            pltpu.VMEM((NS, K, S), F32),
            pltpu.VMEM((NS, K, S), F32),
            pltpu.VMEM((8, S), F32),
            pltpu.VMEM((8, S), F32),
            pltpu.VMEM((8, S), F32),
            pltpu.VMEM((8, S), F32),
            pltpu.VMEM((8, S), F32),
            pltpu.VMEM((NT, S), F32),
            pltpu.VMEM((NS, S), F32),
            pltpu.VMEM((NT, S), F32),
            pltpu.VMEM((NS, S), F32),
            pltpu.VMEM((NT, S), F32),
            dma((4,)),
            dma((NS // CHUNK,)),
            regular((NZ,)),
            regular((NX,)),
            regular((NT,)),
            dma((NZ,)),
            dma((NZ,)),
            dma((NZ,)),
            dma((NZ,)),
            dma((NZ,)),
            dma((NZ,)),
            dma((NZ,)),
            dma((1,)),
            dma((1,)),
            dma((5,)),
            dma((5,)),
        ],
        compiler_params=pltpu.CompilerParams(collective_id=0, has_side_effects=True),
        name="davidson",
    )(
        trial_vectors.reshape(K, S),
        couplings.reshape(NS, S, S),
        neighbours.reshape(1, NS),
        live_slots.reshape(1, NS),
        energies,
    )
    sigma, residual, norms = pl.pallas_call(
        finish,
        out_shape=(
            jax.ShapeDtypeStruct((K, S), F32),
            jax.ShapeDtypeStruct((K, S), F32),
            jax.ShapeDtypeStruct((1, K), F32),
        ),
        in_specs=[vmem],
        out_specs=(vmem, vmem, vmem),
        name="finish",
    )(packed)
    return sigma.reshape(K, 1, S), residual.reshape(K, 1, S), norms.reshape(K)


def solution(mesh):
    return jax.shard_map(
        shards,
        mesh=mesh,
        in_specs=(
            P(None, ("tgt", "src"), None),
            P("tgt", "src", None, None),
            P("tgt", "src"),
            P("tgt", "src"),
            P(("tgt", "src"), None),
        ),
        out_specs=(P(None, ("tgt", "src"), None), P(None, ("tgt", "src"), None), P()),
        check_vma=False,
    )
```

```python
import functools

import jax
import jax.numpy as jnp
from jax import lax
from jax.experimental import pallas as pl
from jax.experimental.pallas import tpu as pltpu
from jax.sharding import PartitionSpec as P

MESH = pl.DeviceIdType.MESH
F32 = jnp.float32
BF16 = jnp.bfloat16
HIGHEST = lax.Precision.HIGHEST

NZ, NX, NT = 8, 4, 16
NS = NZ * NX
K, S = 8, 128
SHIFT = 2.0
CHUNK = 8
NT_DIMS = (((1,), (1,)), ((), ()))


def remote(src, dst, send_sem, recv_sem, device):
    return pltpu.make_async_remote_copy(
        src_ref=src,
        dst_ref=dst,
        send_sem=send_sem,
        recv_sem=recv_sem,
        device_id=device,
        device_id_type=MESH,
    )


def drain(ref, sem):
    pltpu.make_async_copy(ref, ref, sem).wait()


def as_row(pairs):
    full = jnp.concatenate([pairs, jnp.zeros_like(pairs)], axis=0)
    return lax.dot_general(
        jnp.ones((8, S), F32), full, NT_DIMS, precision=HIGHEST, preferred_element_type=F32
    )


def as_row8(tile):
    full = jnp.concatenate([tile, jnp.zeros((S - K, S), F32)], axis=0)
    return lax.dot_general(
        jnp.ones((8, S), F32), full, NT_DIMS, precision=HIGHEST, preferred_element_type=F32
    )


def as_tile(row):
    return pltpu.roll(jnp.broadcast_to(row, (K, S)), S - K * (K - 1), 1, stride=K, stride_axis=0)


def kernel(
    trial_hbm,
    couplings_hbm,
    neighbours_hbm,
    live_hbm,
    energies_hbm,
    packed_ref,
    own,
    energy,
    raw,
    halves,
    index,
    live,
    rows,
    parts,
    sums,
    row_p,
    row_g,
    row_q,
    row_s,
    row_u,
    tgt_p,
    plane_p,
    tgt_g,
    plane_s,
    tgt_s,
    load_sem,
    chunk_sem,
    z_send,
    z_recv,
    x_send,
    x_recv,
    part_send,
    part_recv,
    small_send,
    small_recv,
):
    t, s = lax.axis_index("tgt"), lax.axis_index("src")
    z, x = s // NX, s % NX

    loads = [
        pltpu.make_async_copy(trial_hbm, own, load_sem.at[0]),
        pltpu.make_async_copy(energies_hbm, energy, load_sem.at[1]),
        pltpu.make_async_copy(neighbours_hbm, index, load_sem.at[2]),
        pltpu.make_async_copy(live_hbm, live, load_sem.at[3]),
    ]
    loads[0].start()

    barrier = pltpu.get_barrier_semaphore()

    def greet(device):
        pl.semaphore_signal(barrier, inc=1, device_id=device, device_id_type=MESH)

    def along_z(d):
        return ((z + d) % NZ) * NX + x

    def along_x(d):
        return z * NX + (x + d) % NX

    def greet_beside(d, _):
        greet(((t + 1) % NT, along_x(d)))
        greet(((t + NT - 1) % NT, along_x(d)))

    lax.fori_loop(1, NZ, lambda d, _: greet((t, along_z(d))), None)
    lax.fori_loop(0, NX, greet_beside, None)
    lax.fori_loop(2, NT - 1, lambda d, _: greet(((t + d) % NT, s)), None)
    lax.fori_loop(1, NX, lambda d, _: greet((t, along_x(d))), None)

    for load in loads[1:]:
        load.start()
    fetches = [
        pltpu.make_async_copy(
            couplings_hbm.at[pl.ds(c * CHUNK, CHUNK)], raw.at[pl.ds(c * CHUNK, CHUNK)], chunk_sem.at[c]
        )
        for c in range(NS // CHUNK)
    ]
    for fetch in fetches:
        fetch.start()
    loads[0].wait()
    pl.semaphore_wait(barrier, NZ - 1 + 2 * NX + NT - 3 + NX - 1)

    block = (t % 2) * NS
    mine = block + s

    def send_z(d, _):
        remote(own, rows.at[mine], z_send.at[0], z_recv.at[z], (t, along_z(d))).start()

    lax.fori_loop(1, NZ, send_z, None)
    here = pltpu.make_async_copy(own, rows.at[mine], load_sem.at[0])
    here.start()

    def forward(src, j):
        at = block + j * NX + x
        beside = (t + NT - 1 + 2 * (j // 4)) % NT

        def send_beside(d, _):
            remote(src, rows.at[at], x_send.at[0], x_recv.at[0], (beside, along_x(d))).start()

        def send_x(d, _):
            remote(src, rows.at[at], x_send.at[0], x_recv.at[0], (t, along_x(d))).start()

        lax.fori_loop(0, NX, send_beside, None)
        lax.fori_loop(1, NX, send_x, None)

    forward(own, z)

    def split(i, _):
        tile = raw[i]
        high = tile.astype(BF16)
        halves[i, :, 0:S] = high
        halves[i, :, S : 2 * S] = (tile - high.astype(F32)).astype(BF16)

    for c, fetch in enumerate(fetches):
        fetch.wait()
        lax.fori_loop(c * CHUNK, (c + 1) * CHUNK, split, None, unroll=2)
    for load in loads[1:]:
        load.wait()
    here.wait()

    for d in (1, 7, 2, 6, 3, 5, 4):
        j = (z + d) % NZ
        row = rows.at[block + j * NX + x]
        drain(row, z_recv.at[j])
        forward(row, j)
    drain(rows.at[pl.ds(0, 2 * NS - NZ)], x_recv.at[0])

    def share(i, _):
        found = rows[index[0, i] % 64] * live[0, i].astype(F32)
        high = found.astype(BF16).astype(F32)
        low = found - high
        left = jnp.concatenate(
            [jnp.concatenate([high, low], 0), jnp.concatenate([high, jnp.zeros_like(high)], 0)], 1
        ).astype(BF16)
        both = lax.dot_general(left, halves[i], NT_DIMS, preferred_element_type=F32)
        parts[i] = both[0:K] + both[K : 2 * K]

    def send_parts(d):
        def send_part(e, _):
            to = ((z + d) % NZ) * NX + (x + e) % NX
            remote(parts.at[to], sums.at[s], part_send.at[0], part_recv.at[0], (t, to)).start()

        lax.fori_loop(0 if d else 1, NX, send_part, None)

    order = (4, 3, 5, 2, 6, 1, 7, 0)
    for n, d in enumerate(order):
        first = ((z + d) % NZ) * NX
        lax.fori_loop(0, NX, lambda e, _: share(first + e, None), None, unroll=True)
        if n:
            send_parts(order[n - 1])

    def outer(pairs, left, right):
        return tuple(
            pairs[l] + left * jnp.broadcast_to(right[l : l + 1], (K, S)) for l in range(K)
        )

    vector = own[...]
    diagonal = vector * (energy[...] - SHIFT)
    zeros = tuple(jnp.zeros((K, S), F32) for _ in range(K))
    pairs = lax.fori_loop(
        0, NS // 2, lambda i, p: outer(p, rows[block + i], parts[i]), zeros, unroll=8
    )
    send_parts(order[-1])
    pairs = lax.fori_loop(
        NS // 2, NS, lambda i, p: outer(p, rows[block + i], parts[i]), pairs, unroll=8
    )
    pairs = outer(pairs, vector, diagonal)
    row_p[...] = as_row(jnp.concatenate(pairs[::-1], 0))

    def send_tgt(src, buf, sem):
        def one(d, _):
            remote(
                src.at[pl.ds(0, 1)],
                buf.at[pl.ds(t, 1)],
                small_send.at[sem],
                small_recv.at[sem],
                ((t + d) % NT, s),
            ).start()

        lax.fori_loop(1, NT, one, None)
        buf[pl.ds(t, 1), :] = src[0:1, :]

    def wait_tgt(buf, sem):
        drain(buf.at[pl.ds(0, NT - 1)], small_recv.at[sem])
        return jnp.sum(buf[...], axis=0, keepdims=True)

    def send_plane(src, buf, sem):
        def one(d, _):
            to = ((z + 4 + d // NX) % NZ) * NX + (x + 2 + d % NX) % NX

            @pl.when(to != s)
            def _():
                remote(
                    src.at[pl.ds(0, 1)],
                    buf.at[pl.ds(s, 1)],
                    small_send.at[sem],
                    small_recv.at[sem],
                    (t, to),
                ).start()

        lax.fori_loop(0, NS, one, None)
        buf[pl.ds(s, 1), :] = src[0:1, :]

    def wait_plane(buf, sem):
        drain(buf.at[pl.ds(0, NS - 1)], small_recv.at[sem])
        return jnp.sum(buf[...], axis=0, keepdims=True)

    send_tgt(row_p, tgt_p, 0)

    def gram(i, p):
        return outer(p, rows[block + i], rows[block + i])

    pairs = lax.fori_loop(0, NS, gram, zeros, unroll=8)
    row_g[...] = as_row(jnp.concatenate(pairs[::-1], 0))
    send_tgt(row_g, tgt_g, 1)

    drain(sums.at[pl.ds(0, NS - 1)], part_recv.at[0])
    sums[s] = parts[s]
    shifted = jnp.sum(sums[...], axis=0) + diagonal
    row_s[...] = as_row8(shifted * shifted)
    send_plane(row_s, plane_s, 3)
    packed_ref[2 * K : 3 * K] = jnp.zeros((K, S), F32)
    packed_ref[0:K] = shifted + SHIFT * vector

    row_q[...] = jnp.broadcast_to(wait_tgt(tgt_p, 0), (8, S))
    send_plane(row_q, plane_p, 2)

    metric = as_tile(wait_tgt(tgt_g, 1))
    lane = lax.broadcasted_iota(jnp.int32, (K, S), 1)
    sub = lax.broadcasted_iota(jnp.int32, (K, S), 0)
    norms2 = jnp.sum(jnp.where(lane == sub, metric, 0.0), axis=0, keepdims=True)
    work = metric
    solved = [vector, jnp.where(lane == sub, 1.0, 0.0)]
    factors = []
    for j in range(K):
        column = jnp.broadcast_to(work[:, j : j + 1], (K, S))
        pivot = lax.rsqrt(jnp.broadcast_to(column[j : j + 1], (K, S)))
        column = jnp.where(sub >= j, column * pivot, 0.0)
        factors.append((column, pivot))
        line = jnp.sum(jnp.where(lane == sub, column, 0.0), axis=0, keepdims=True)
        work = work - column * jnp.broadcast_to(line, (K, S))
        for n in range(2):
            top = jnp.broadcast_to(solved[n][j : j + 1], (K, S)) * pivot
            below = solved[n] - jnp.where(sub > j, column * top, 0.0)
            solved[n] = jnp.where(sub == j, top, below)
    for j in reversed(range(K)):
        column, pivot = factors[j]
        for n in range(2):
            dots = jnp.sum(jnp.where(sub > j, column * solved[n], 0.0), axis=0, keepdims=True)
            value = (solved[n] - jnp.broadcast_to(dots, (K, S))) * pivot
            solved[n] = jnp.where(sub == j, value, solved[n])
    solved, inverse = solved

    row_u[...] = jnp.broadcast_to(wait_plane(plane_s, 3), (8, S))
    send_tgt(row_u, tgt_s, 4)

    def times(left, right):
        total = jnp.zeros((K, S), F32)
        for j in range(K):
            total = total + jnp.broadcast_to(left[:, j : j + 1], (K, S)) * jnp.broadcast_to(
                right[j : j + 1], (K, S)
            )
        return total

    projected = as_tile(wait_plane(plane_p, 2))
    packed_ref[K : 2 * K] = shifted - times(projected, solved)
    square_mesh = (lane < K) & (sub < K)
    mixing = times(projected, inverse)
    missing = projected - times(mixing, metric)
    taken = as_row8(jnp.where(square_mesh, mixing * (projected + missing), 0.0))

    left_over = jnp.maximum(wait_tgt(tgt_s, 4) - taken[0:1], 0.0)
    packed_ref[2 * K : 2 * K + 1] = jnp.sqrt(left_over / jnp.where(lane[0:1] < K, norms2, 1.0))

    drain(rows.at[pl.ds(0, NZ - 1)], z_send.at[0])
    drain(rows.at[pl.ds(0, 2 * NS - NZ)], x_send.at[0])
    drain(parts.at[pl.ds(0, NS - 1)], part_send.at[0])
    for sem, buf, count in ((0, tgt_p, NT), (1, tgt_g, NT), (2, plane_p, NS), (3, plane_s, NS), (4, tgt_s, NT)):
        drain(buf.at[pl.ds(0, count - 1)], small_send.at[sem])


def finish(packed_ref, sigma_ref, residual_ref, norms_ref):
    sigma_ref[...] = packed_ref[0:K]
    residual_ref[...] = packed_ref[K : 2 * K]
    norms_ref[...] = packed_ref[2 * K : 2 * K + 1, 0:K]


def shards(trial_vectors, couplings, neighbours, live_slots, energies):
    hbm = pl.BlockSpec(memory_space=pltpu.HBM)
    vmem = pl.BlockSpec(memory_space=pltpu.VMEM)
    dma = pltpu.SemaphoreType.DMA
    packed = pl.pallas_call(
        kernel,
        out_shape=jax.ShapeDtypeStruct((3 * K, S), F32),
        in_specs=[hbm] * 5,
        out_specs=vmem,
        scratch_shapes=[
            pltpu.VMEM((K, S), F32),
            pltpu.VMEM((1, S), F32),
            pltpu.VMEM((NS, S, S), F32),
            pltpu.VMEM((NS, S, 2 * S), BF16),
            pltpu.SMEM((1, NS), jnp.int32),
            pltpu.SMEM((1, NS), jnp.int32),
            pltpu.VMEM((64, K, S), F32),
            pltpu.VMEM((NS, K, S), F32),
            pltpu.VMEM((NS, K, S), F32),
            pltpu.VMEM((8, S), F32),
            pltpu.VMEM((8, S), F32),
            pltpu.VMEM((8, S), F32),
            pltpu.VMEM((8, S), F32),
            pltpu.VMEM((8, S), F32),
            pltpu.VMEM((NT, S), F32),
            pltpu.VMEM((NS, S), F32),
            pltpu.VMEM((NT, S), F32),
            pltpu.VMEM((NS, S), F32),
            pltpu.VMEM((NT, S), F32),
            dma((4,)),
            dma((NS // CHUNK,)),
            dma((1,)),
            dma((NZ,)),
            dma((1,)),
            dma((1,)),
            dma((1,)),
            dma((1,)),
            dma((5,)),
            dma((5,)),
        ],
        compiler_params=pltpu.CompilerParams(collective_id=0, has_side_effects=True),
        name="davidson",
    )(
        trial_vectors.reshape(K, S),
        couplings.reshape(NS, S, S),
        neighbours.reshape(1, NS),
        live_slots.reshape(1, NS),
        energies,
    )
    sigma, residual, norms = pl.pallas_call(
        finish,
        out_shape=(
            jax.ShapeDtypeStruct((K, S), F32),
            jax.ShapeDtypeStruct((K, S), F32),
            jax.ShapeDtypeStruct((1, K), F32),
        ),
        in_specs=[vmem],
        out_specs=(vmem, vmem, vmem),
        name="finish",
    )(packed)
    return sigma.reshape(K, 1, S), residual.reshape(K, 1, S), norms.reshape(K)


def solution(mesh):
    return jax.shard_map(
        shards,
        mesh=mesh,
        in_specs=(
            P(None, ("tgt", "src"), None),
            P("tgt", "src", None, None),
            P("tgt", "src"),
            P("tgt", "src"),
            P(("tgt", "src"), None),
        ),
        out_specs=(P(None, ("tgt", "src"), None), P(None, ("tgt", "src"), None), P()),
        check_vma=False,
    )
```

```python
import functools

import jax
import jax.numpy as jnp
from jax import lax
from jax.experimental import pallas as pl
from jax.experimental.pallas import tpu as pltpu
from jax.sharding import PartitionSpec as P

MESH = pl.DeviceIdType.MESH
F32 = jnp.float32
BF16 = jnp.bfloat16
HIGHEST = lax.Precision.HIGHEST

NZ, NX, NT = 8, 4, 16
NS = NZ * NX
K, S = 8, 128
SHIFT = 2.0
CHUNK = 8
NT_DIMS = (((1,), (1,)), ((), ()))


def remote(src, dst, send_sem, recv_sem, device):
    return pltpu.make_async_remote_copy(
        src_ref=src,
        dst_ref=dst,
        send_sem=send_sem,
        recv_sem=recv_sem,
        device_id=device,
        device_id_type=MESH,
    )


def drain(ref, sem):
    pltpu.make_async_copy(ref, ref, sem).wait()


def far_first(n, count):
    return count // 2 + (1 - 2 * (n % 2)) * ((n + 1) // 2)


def as_row(pairs):
    full = jnp.concatenate([pairs, jnp.zeros_like(pairs)], axis=0)
    return lax.dot_general(
        jnp.ones((8, S), F32), full, NT_DIMS, precision=HIGHEST, preferred_element_type=F32
    )


def as_row8(tile):
    total = jnp.broadcast_to(jnp.sum(tile, axis=1, keepdims=True), (K, S))
    lane = lax.broadcasted_iota(jnp.int32, (K, S), 1)
    sub = lax.broadcasted_iota(jnp.int32, (K, S), 0)
    return jnp.sum(jnp.where(lane == sub, total, 0.0), axis=0, keepdims=True)


def as_tile(row):
    return pltpu.roll(jnp.broadcast_to(row, (K, S)), S - K * (K - 1), 1, stride=K, stride_axis=0)


def kernel(
    trial_hbm,
    couplings_hbm,
    neighbours_hbm,
    live_hbm,
    energies_hbm,
    packed_ref,
    own,
    energy,
    raw,
    halves,
    index,
    live,
    rows,
    parts,
    sums,
    row_p,
    row_g,
    row_q,
    row_s,
    row_u,
    tgt_p,
    plane_p,
    tgt_g,
    plane_s,
    tgt_s,
    load_sem,
    chunk_sem,
    z_send,
    z_recv,
    x_send,
    x_recv,
    part_send,
    part_recv,
    small_send,
    small_recv,
):
    t, s = lax.axis_index("tgt"), lax.axis_index("src")
    z, x = s // NX, s % NX

    loads = [
        pltpu.make_async_copy(trial_hbm, own, load_sem.at[0]),
        pltpu.make_async_copy(energies_hbm, energy, load_sem.at[1]),
        pltpu.make_async_copy(neighbours_hbm, index, load_sem.at[2]),
        pltpu.make_async_copy(live_hbm, live, load_sem.at[3]),
    ]
    loads[0].start()

    barrier = pltpu.get_barrier_semaphore()

    def greet(device):
        pl.semaphore_signal(barrier, inc=1, device_id=device, device_id_type=MESH)

    def along_z(d):
        return ((z + d) % NZ) * NX + x

    def along_x(d):
        return z * NX + (x + d) % NX

    def greet_beside(d, _):
        greet(((t + 1) % NT, along_x(d)))
        greet(((t + NT - 1) % NT, along_x(d)))

    lax.fori_loop(0, NZ - 1, lambda n, _: greet((t, along_z(far_first(n, NZ)))), None, unroll=True)
    lax.fori_loop(0, NT - 3, lambda n, _: greet(((t + far_first(n, NT)) % NT, s)), None, unroll=True)
    lax.fori_loop(0, NX, greet_beside, None, unroll=True)
    lax.fori_loop(1, NX, lambda d, _: greet((t, along_x(d))), None, unroll=True)

    for load in loads[1:]:
        load.start()
    fetches = [
        pltpu.make_async_copy(
            couplings_hbm.at[pl.ds(c * CHUNK, CHUNK)], raw.at[pl.ds(c * CHUNK, CHUNK)], chunk_sem.at[c]
        )
        for c in range(NS // CHUNK)
    ]
    for fetch in fetches:
        fetch.start()
    loads[0].wait()
    pl.semaphore_wait(barrier, NZ - 1 + 2 * NX + NT - 3 + NX - 1)

    block = (t % 2) * NS
    mine = block + s

    def send_z(n, _):
        to = (t, along_z(far_first(n, NZ)))
        remote(own, rows.at[mine], z_send.at[0], z_recv.at[z], to).start()

    lax.fori_loop(0, NZ - 1, send_z, None, unroll=True)
    here = pltpu.make_async_copy(own, rows.at[mine], load_sem.at[0])
    here.start()

    def forward(src, j):
        at = block + j * NX + x
        beside = (t + NT - 1 + 2 * (j // 4)) % NT

        for n in range(NX):
            to = along_x(far_first(n, NX))
            for plane in (beside, t) if n < NX - 1 else (beside,):
                remote(src, rows.at[at], x_send.at[0], x_recv.at[0], (plane, to)).start()

    forward(own, z)

    def split(i, _):
        tile = raw[i]
        high = tile.astype(BF16)
        halves[i, :, 0:S] = high
        halves[i, :, S : 2 * S] = (tile - high.astype(F32)).astype(BF16)

    for c, fetch in enumerate(fetches):
        fetch.wait()
        lax.fori_loop(c * CHUNK, (c + 1) * CHUNK, split, None, unroll=2)
    for load in loads[1:]:
        load.wait()
    here.wait()

    for d in (1, 7, 2, 6, 3, 5, 4):
        j = (z + d) % NZ
        row = rows.at[block + j * NX + x]
        drain(row, z_recv.at[j])
        forward(row, j)
    drain(rows.at[pl.ds(0, 2 * NS - NZ)], x_recv.at[0])

    def share(i, _):
        found = rows[index[0, i] % 64] * live[0, i].astype(F32)
        high = found.astype(BF16).astype(F32)
        low = found - high
        left = jnp.concatenate(
            [jnp.concatenate([high, low], 0), jnp.concatenate([high, jnp.zeros_like(high)], 0)], 1
        ).astype(BF16)
        both = lax.dot_general(left, halves[i], NT_DIMS, preferred_element_type=F32)
        parts[i] = both[0:K] + both[K : 2 * K]

    def send_parts(d):
        def send_part(e, _):
            to = ((z + d) % NZ) * NX + (x + e) % NX
            remote(parts.at[to], sums.at[s], part_send.at[0], part_recv.at[0], (t, to)).start()

        lax.fori_loop(0 if d else 1, NX, send_part, None)

    order = (4, 3, 5, 2, 6, 1, 7, 0)
    for n, d in enumerate(order):
        first = ((z + d) % NZ) * NX
        lax.fori_loop(0, NX, lambda e, _: share(first + e, None), None, unroll=True)
        if n:
            send_parts(order[n - 1])

    def outer(pairs, left, right):
        return tuple(
            pairs[l] + left * jnp.broadcast_to(right[l : l + 1], (K, S)) for l in range(K)
        )

    vector = own[...]
    diagonal = vector * (energy[...] - SHIFT)
    zeros = tuple(jnp.zeros((K, S), F32) for _ in range(K))
    pairs = lax.fori_loop(
        0, NS // 2, lambda i, p: outer(p, rows[block + i], parts[i]), zeros, unroll=8
    )
    send_parts(order[-1])
    pairs = lax.fori_loop(
        NS // 2, NS, lambda i, p: outer(p, rows[block + i], parts[i]), pairs, unroll=8
    )
    pairs = outer(pairs, vector, diagonal)
    row_p[...] = as_row(jnp.concatenate(pairs[::-1], 0))

    def send_tgt(src, buf, sem):
        def one(n, _):
            remote(
                src.at[pl.ds(0, 1)],
                buf.at[pl.ds(t, 1)],
                small_send.at[sem],
                small_recv.at[sem],
                ((t + far_first(n, NT)) % NT, s),
            ).start()

        lax.fori_loop(0, NT - 1, one, None, unroll=True)
        buf[pl.ds(t, 1), :] = src[0:1, :]

    def wait_tgt(buf, sem):
        drain(buf.at[pl.ds(0, NT - 1)], small_recv.at[sem])
        return jnp.sum(buf[...], axis=0, keepdims=True)

    def send_plane(src, buf, sem):
        def one(n, _):
            to_z = (z + far_first(n // NX, NZ)) % NZ
            to_x = (x + far_first(n % NX, NX)) % NX
            remote(
                src.at[pl.ds(0, 1)],
                buf.at[pl.ds(s, 1)],
                small_send.at[sem],
                small_recv.at[sem],
                (t, to_z * NX + to_x),
            ).start()

        lax.fori_loop(0, NS - 1, one, None, unroll=True)
        buf[pl.ds(s, 1), :] = src[0:1, :]

    def wait_plane(buf, sem):
        drain(buf.at[pl.ds(0, NS - 1)], small_recv.at[sem])
        return jnp.sum(buf[...], axis=0, keepdims=True)

    send_tgt(row_p, tgt_p, 0)

    def gram(i, p):
        return outer(p, rows[block + i], rows[block + i])

    pairs = lax.fori_loop(0, NS, gram, zeros, unroll=8)
    row_g[...] = as_row(jnp.concatenate(pairs[::-1], 0))
    send_tgt(row_g, tgt_g, 1)

    drain(sums.at[pl.ds(0, NS - 1)], part_recv.at[0])
    sums[s] = parts[s]
    shifted = jnp.sum(sums[...], axis=0) + diagonal
    row_s[...] = jnp.broadcast_to(as_row8(shifted * shifted), (8, S))
    send_plane(row_s, plane_s, 3)
    packed_ref[2 * K : 3 * K] = jnp.zeros((K, S), F32)
    packed_ref[0:K] = shifted + SHIFT * vector

    row_q[...] = jnp.broadcast_to(wait_tgt(tgt_p, 0), (8, S))
    send_plane(row_q, plane_p, 2)

    metric = as_tile(wait_tgt(tgt_g, 1))
    lane = lax.broadcasted_iota(jnp.int32, (K, S), 1)
    sub = lax.broadcasted_iota(jnp.int32, (K, S), 0)
    norms2 = jnp.sum(jnp.where(lane == sub, metric, 0.0), axis=0, keepdims=True)
    work = metric
    solved = [vector, jnp.where(lane == sub, 1.0, 0.0)]
    factors = []
    for j in range(K):
        column = jnp.broadcast_to(work[:, j : j + 1], (K, S))
        pivot = lax.rsqrt(jnp.broadcast_to(column[j : j + 1], (K, S)))
        column = jnp.where(sub >= j, column * pivot, 0.0)
        factors.append((column, pivot))
        line = jnp.sum(jnp.where(lane == sub, column, 0.0), axis=0, keepdims=True)
        work = work - column * jnp.broadcast_to(line, (K, S))
        for n in range(2):
            top = jnp.broadcast_to(solved[n][j : j + 1], (K, S)) * pivot
            below = solved[n] - jnp.where(sub > j, column * top, 0.0)
            solved[n] = jnp.where(sub == j, top, below)
    for j in reversed(range(K)):
        column, pivot = factors[j]
        for n in range(2):
            dots = jnp.sum(jnp.where(sub > j, column * solved[n], 0.0), axis=0, keepdims=True)
            value = (solved[n] - jnp.broadcast_to(dots, (K, S))) * pivot
            solved[n] = jnp.where(sub == j, value, solved[n])
    solved, inverse = solved

    row_u[...] = jnp.broadcast_to(wait_plane(plane_s, 3), (8, S))
    send_tgt(row_u, tgt_s, 4)

    def times(left, right):
        total = jnp.zeros((K, S), F32)
        for j in range(K):
            total = total + jnp.broadcast_to(left[:, j : j + 1], (K, S)) * jnp.broadcast_to(
                right[j : j + 1], (K, S)
            )
        return total

    projected = as_tile(wait_plane(plane_p, 2))
    packed_ref[K : 2 * K] = shifted - times(projected, solved)
    square_mesh = (lane < K) & (sub < K)
    mixing = times(projected, inverse)
    missing = projected - times(mixing, metric)
    taken = as_row8(jnp.where(square_mesh, mixing * (projected + missing), 0.0))

    left_over = jnp.maximum(wait_tgt(tgt_s, 4) - taken, 0.0)
    packed_ref[2 * K : 2 * K + 1] = jnp.sqrt(left_over / jnp.where(lane[0:1] < K, norms2, 1.0))

    drain(rows.at[pl.ds(0, NZ - 1)], z_send.at[0])
    drain(rows.at[pl.ds(0, 2 * NS - NZ)], x_send.at[0])
    drain(parts.at[pl.ds(0, NS - 1)], part_send.at[0])
    for sem, buf, count in ((0, tgt_p, NT), (1, tgt_g, NT), (2, plane_p, NS), (3, plane_s, NS), (4, tgt_s, NT)):
        drain(buf.at[pl.ds(0, count - 1)], small_send.at[sem])


def finish(packed_ref, sigma_ref, residual_ref, norms_ref):
    sigma_ref[...] = packed_ref[0:K]
    residual_ref[...] = packed_ref[K : 2 * K]
    norms_ref[...] = packed_ref[2 * K : 2 * K + 1, 0:K]


def shards(trial_vectors, couplings, neighbours, live_slots, energies):
    hbm = pl.BlockSpec(memory_space=pltpu.HBM)
    vmem = pl.BlockSpec(memory_space=pltpu.VMEM)
    dma = pltpu.SemaphoreType.DMA
    packed = pl.pallas_call(
        kernel,
        out_shape=pltpu.VMEM((3 * K, S), F32),
        in_specs=[hbm] * 5,
        out_specs=vmem,
        scratch_shapes=[
            pltpu.VMEM((K, S), F32),
            pltpu.VMEM((1, S), F32),
            pltpu.VMEM((NS, S, S), F32),
            pltpu.VMEM((NS, S, 2 * S), BF16),
            pltpu.SMEM((1, NS), jnp.int32),
            pltpu.SMEM((1, NS), jnp.int32),
            pltpu.VMEM((64, K, S), F32),
            pltpu.VMEM((NS, K, S), F32),
            pltpu.VMEM((NS, K, S), F32),
            pltpu.VMEM((8, S), F32),
            pltpu.VMEM((8, S), F32),
            pltpu.VMEM((8, S), F32),
            pltpu.VMEM((8, S), F32),
            pltpu.VMEM((8, S), F32),
            pltpu.VMEM((NT, S), F32),
            pltpu.VMEM((NS, S), F32),
            pltpu.VMEM((NT, S), F32),
            pltpu.VMEM((NS, S), F32),
            pltpu.VMEM((NT, S), F32),
            dma((4,)),
            dma((NS // CHUNK,)),
            dma((1,)),
            dma((NZ,)),
            dma((1,)),
            dma((1,)),
            dma((1,)),
            dma((1,)),
            dma((5,)),
            dma((5,)),
        ],
        compiler_params=pltpu.CompilerParams(collective_id=0, has_side_effects=True),
        name="davidson",
    )(
        trial_vectors.reshape(K, S),
        couplings.reshape(NS, S, S),
        neighbours.reshape(1, NS),
        live_slots.reshape(1, NS),
        energies,
    )
    sigma, residual, norms = pl.pallas_call(
        finish,
        out_shape=(
            jax.ShapeDtypeStruct((K, S), F32),
            jax.ShapeDtypeStruct((K, S), F32),
            jax.ShapeDtypeStruct((1, K), F32),
        ),
        in_specs=[vmem],
        out_specs=(vmem, vmem, vmem),
        name="finish",
    )(pltpu.with_memory_space_constraint(packed, pltpu.VMEM))
    return sigma.reshape(K, 1, S), residual.reshape(K, 1, S), norms.reshape(K)


def solution(mesh):
    return jax.shard_map(
        shards,
        mesh=mesh,
        in_specs=(
            P(None, ("tgt", "src"), None),
            P("tgt", "src", None, None),
            P("tgt", "src"),
            P("tgt", "src"),
            P(("tgt", "src"), None),
        ),
        out_specs=(P(None, ("tgt", "src"), None), P(None, ("tgt", "src"), None), P()),
        check_vma=False,
    )
```

```python
import functools

import jax
import jax.numpy as jnp
from jax import lax
from jax.experimental import pallas as pl
from jax.experimental.pallas import tpu as pltpu
from jax.sharding import PartitionSpec as P

MESH = pl.DeviceIdType.MESH
F32 = jnp.float32
BF16 = jnp.bfloat16
HIGHEST = lax.Precision.HIGHEST

NZ, NX, NT = 8, 4, 16
NS = NZ * NX
K, S = 8, 128
SHIFT = 2.0
CHUNK = 8
NT_DIMS = (((1,), (1,)), ((), ()))


def remote(src, dst, send_sem, recv_sem, device):
    return pltpu.make_async_remote_copy(
        src_ref=src,
        dst_ref=dst,
        send_sem=send_sem,
        recv_sem=recv_sem,
        device_id=device,
        device_id_type=MESH,
    )


def drain(ref, sem):
    pltpu.make_async_copy(ref, ref, sem).wait()


def far_first(n, count):
    return count // 2 + (1 - 2 * (n % 2)) * ((n + 1) // 2)


def as_row(pairs):
    full = jnp.concatenate([pairs, jnp.zeros_like(pairs)], axis=0)
    return lax.dot_general(
        jnp.ones((8, S), F32), full, NT_DIMS, precision=HIGHEST, preferred_element_type=F32
    )


def as_row8(tile):
    total = jnp.broadcast_to(jnp.sum(tile, axis=1, keepdims=True), (K, S))
    lane = lax.broadcasted_iota(jnp.int32, (K, S), 1)
    sub = lax.broadcasted_iota(jnp.int32, (K, S), 0)
    return jnp.sum(jnp.where(lane == sub, total, 0.0), axis=0, keepdims=True)


def as_tile(row):
    return pltpu.roll(jnp.broadcast_to(row, (K, S)), S - K * (K - 1), 1, stride=K, stride_axis=0)


def kernel(
    trial_hbm,
    couplings_hbm,
    neighbours_hbm,
    live_hbm,
    energies_hbm,
    packed_ref,
    own,
    energy,
    raw,
    halves,
    index,
    live,
    rows,
    parts,
    sums,
    row_p,
    row_g,
    row_q,
    row_s,
    row_u,
    tgt_p,
    plane_p,
    tgt_g,
    plane_s,
    tgt_s,
    load_sem,
    chunk_sem,
    z_send,
    z_recv,
    x_send,
    x_recv,
    part_send,
    part_recv,
    small_send,
    small_recv,
):
    t, s = lax.axis_index("tgt"), lax.axis_index("src")
    z, x = s // NX, s % NX

    loads = [
        pltpu.make_async_copy(trial_hbm, own, load_sem.at[0]),
        pltpu.make_async_copy(energies_hbm, energy, load_sem.at[1]),
        pltpu.make_async_copy(neighbours_hbm, index, load_sem.at[2]),
        pltpu.make_async_copy(live_hbm, live, load_sem.at[3]),
    ]
    loads[0].start()

    barrier = pltpu.get_barrier_semaphore()

    def greet(device):
        pl.semaphore_signal(barrier, inc=1, device_id=device, device_id_type=MESH)

    def along_z(d):
        return lax.rem(z + d, NZ) * NX + x

    def along_x(d):
        return z * NX + lax.rem(x + d, NX)

    def greet_beside(d, _):
        greet((lax.rem(t + 1, NT), along_x(d)))
        greet((lax.rem(t + NT - 1, NT), along_x(d)))

    lax.fori_loop(0, NZ - 1, lambda n, _: greet((t, along_z(far_first(n, NZ)))), None, unroll=True)
    lax.fori_loop(0, NT - 3, lambda n, _: greet((lax.rem(t + far_first(n, NT), NT), s)), None, unroll=True)
    lax.fori_loop(0, NX, greet_beside, None, unroll=True)
    lax.fori_loop(1, NX, lambda d, _: greet((t, along_x(d))), None, unroll=True)

    for load in loads[1:]:
        load.start()
    fetches = [
        pltpu.make_async_copy(
            couplings_hbm.at[pl.ds(c * CHUNK, CHUNK)], raw.at[pl.ds(c * CHUNK, CHUNK)], chunk_sem.at[c]
        )
        for c in range(NS // CHUNK)
    ]
    for fetch in fetches:
        fetch.start()
    loads[0].wait()
    pl.semaphore_wait(barrier, NZ - 1 + 2 * NX + NT - 3 + NX - 1)

    block = (t % 2) * NS
    mine = block + s

    def send_z(n, _):
        to = (t, along_z(far_first(n, NZ)))
        remote(own, rows.at[mine], z_send.at[0], z_recv.at[z], to).start()

    lax.fori_loop(0, NZ - 1, send_z, None, unroll=True)
    here = pltpu.make_async_copy(own, rows.at[mine], load_sem.at[0])
    here.start()

    def forward(src, j):
        at = block + j * NX + x
        beside = (t + NT - 1 + 2 * (j // 4)) % NT

        for n in range(NX):
            to = along_x(far_first(n, NX))
            for plane in (beside, t) if n < NX - 1 else (beside,):
                remote(src, rows.at[at], x_send.at[0], x_recv.at[0], (plane, to)).start()

    forward(own, z)

    def split(i, _):
        tile = raw[i]
        high = tile.astype(BF16)
        halves[i, :, 0:S] = high
        halves[i, :, S : 2 * S] = (tile - high.astype(F32)).astype(BF16)

    for c, fetch in enumerate(fetches):
        fetch.wait()
        lax.fori_loop(c * CHUNK, (c + 1) * CHUNK, split, None, unroll=2)
    for load in loads[1:]:
        load.wait()
    here.wait()

    for d in (1, 7, 2, 6, 3, 5, 4):
        j = (z + d) % NZ
        row = rows.at[block + j * NX + x]
        drain(row, z_recv.at[j])
        forward(row, j)
    drain(rows.at[pl.ds(0, 2 * NS - NZ)], x_recv.at[0])

    def target(n):
        to_z = lax.rem(z + far_first(n // NX, NZ), NZ)
        return to_z * NX + lax.rem(x + far_first(n % NX, NX), NX)

    def share(n, _):
        i = target(n)
        found = rows[lax.rem(index[0, i], 64)] * live[0, i].astype(F32)
        high = found.astype(BF16).astype(F32)
        low = found - high
        left = jnp.concatenate(
            [jnp.concatenate([high, low], 0), jnp.concatenate([high, jnp.zeros_like(high)], 0)], 1
        ).astype(BF16)
        both = lax.dot_general(left, halves[i], NT_DIMS, preferred_element_type=F32)
        parts[i] = both[0:K] + both[K : 2 * K]

    def send_part(n, _):
        to = target(n)
        remote(parts.at[to], sums.at[s], part_send.at[0], part_recv.at[0], (t, to)).start()

    for first in range(0, NS, 8):
        lax.fori_loop(first, first + 8, share, None, unroll=True)
        lax.fori_loop(first, min(first + 8, NS - 1), send_part, None, unroll=True)

    def outer(pairs, left, right):
        return tuple(
            pairs[l] + left * jnp.broadcast_to(right[l : l + 1], (K, S)) for l in range(K)
        )

    vector = own[...]
    diagonal = vector * (energy[...] - SHIFT)
    zeros = tuple(jnp.zeros((K, S), F32) for _ in range(K))
    pairs = lax.fori_loop(
        0, NS // 2, lambda i, p: outer(p, rows[block + i], parts[i]), zeros, unroll=8
    )
    pairs = lax.fori_loop(
        NS // 2, NS, lambda i, p: outer(p, rows[block + i], parts[i]), pairs, unroll=8
    )
    pairs = outer(pairs, vector, diagonal)
    row_p[...] = as_row(jnp.concatenate(pairs[::-1], 0))

    def send_tgt(src, buf, sem):
        def one(n, _):
            remote(
                src.at[pl.ds(0, 1)],
                buf.at[pl.ds(t, 1)],
                small_send.at[sem],
                small_recv.at[sem],
                (lax.rem(t + far_first(n, NT), NT), s),
            ).start()

        lax.fori_loop(0, NT - 1, one, None, unroll=True)
        buf[pl.ds(t, 1), :] = src[0:1, :]

    def wait_tgt(buf, sem):
        drain(buf.at[pl.ds(0, NT - 1)], small_recv.at[sem])
        return jnp.sum(buf[...], axis=0, keepdims=True)

    def send_plane(src, buf, sem):
        def one(n, _):
            to_z = lax.rem(z + far_first(n // NX, NZ), NZ)
            to_x = lax.rem(x + far_first(n % NX, NX), NX)
            remote(
                src.at[pl.ds(0, 1)],
                buf.at[pl.ds(s, 1)],
                small_send.at[sem],
                small_recv.at[sem],
                (t, to_z * NX + to_x),
            ).start()

        lax.fori_loop(0, NS - 1, one, None, unroll=True)
        buf[pl.ds(s, 1), :] = src[0:1, :]

    def wait_plane(buf, sem):
        drain(buf.at[pl.ds(0, NS - 1)], small_recv.at[sem])
        return jnp.sum(buf[...], axis=0, keepdims=True)

    send_tgt(row_p, tgt_p, 0)

    def gram(i, p):
        return outer(p, rows[block + i], rows[block + i])

    pairs = lax.fori_loop(0, NS, gram, zeros, unroll=8)
    row_g[...] = as_row(jnp.concatenate(pairs[::-1], 0))
    send_tgt(row_g, tgt_g, 1)

    drain(sums.at[pl.ds(0, NS - 1)], part_recv.at[0])
    sums[s] = parts[s]
    shifted = jnp.sum(sums[...], axis=0) + diagonal
    row_s[...] = jnp.broadcast_to(as_row8(shifted * shifted), (8, S))
    send_plane(row_s, plane_s, 3)
    packed_ref[2 * K : 3 * K] = jnp.zeros((K, S), F32)
    packed_ref[0:K] = shifted + SHIFT * vector

    row_q[...] = jnp.broadcast_to(wait_tgt(tgt_p, 0), (8, S))
    send_plane(row_q, plane_p, 2)

    metric = as_tile(wait_tgt(tgt_g, 1))
    lane = lax.broadcasted_iota(jnp.int32, (K, S), 1)
    sub = lax.broadcasted_iota(jnp.int32, (K, S), 0)
    norms2 = jnp.sum(jnp.where(lane == sub, metric, 0.0), axis=0, keepdims=True)
    work = metric
    solved = [vector, jnp.where(lane == sub, 1.0, 0.0)]
    factors = []
    for j in range(K):
        column = jnp.broadcast_to(work[:, j : j + 1], (K, S))
        pivot = lax.rsqrt(jnp.broadcast_to(column[j : j + 1], (K, S)))
        column = jnp.where(sub >= j, column * pivot, 0.0)
        factors.append((column, pivot))
        line = jnp.sum(jnp.where(lane == sub, column, 0.0), axis=0, keepdims=True)
        work = work - column * jnp.broadcast_to(line, (K, S))
        for n in range(2):
            top = jnp.broadcast_to(solved[n][j : j + 1], (K, S)) * pivot
            below = solved[n] - jnp.where(sub > j, column * top, 0.0)
            solved[n] = jnp.where(sub == j, top, below)
    for j in reversed(range(K)):
        column, pivot = factors[j]
        for n in range(2):
            dots = jnp.sum(jnp.where(sub > j, column * solved[n], 0.0), axis=0, keepdims=True)
            value = (solved[n] - jnp.broadcast_to(dots, (K, S))) * pivot
            solved[n] = jnp.where(sub == j, value, solved[n])
    solved, inverse = solved

    row_u[...] = jnp.broadcast_to(wait_plane(plane_s, 3), (8, S))
    send_tgt(row_u, tgt_s, 4)

    def times(left, right):
        total = jnp.zeros((K, S), F32)
        for j in range(K):
            total = total + jnp.broadcast_to(left[:, j : j + 1], (K, S)) * jnp.broadcast_to(
                right[j : j + 1], (K, S)
            )
        return total

    projected = as_tile(wait_plane(plane_p, 2))
    packed_ref[K : 2 * K] = shifted - times(projected, solved)
    square_mesh = (lane < K) & (sub < K)
    mixing = times(projected, inverse)
    missing = projected - times(mixing, metric)
    taken = as_row8(jnp.where(square_mesh, mixing * (projected + missing), 0.0))

    scale = 1.0 / jnp.where(lane[0:1] < K, norms2, 1.0)

    drain(rows.at[pl.ds(0, NZ - 1)], z_send.at[0])
    drain(rows.at[pl.ds(0, 2 * NS - NZ)], x_send.at[0])
    drain(parts.at[pl.ds(0, NS - 1)], part_send.at[0])
    for sem, buf, count in ((0, tgt_p, NT), (1, tgt_g, NT), (2, plane_p, NS), (3, plane_s, NS)):
        drain(buf.at[pl.ds(0, count - 1)], small_send.at[sem])

    left_over = jnp.maximum(wait_tgt(tgt_s, 4) - taken, 0.0)
    packed_ref[2 * K : 2 * K + 1] = jnp.sqrt(left_over * scale)
    drain(tgt_s.at[pl.ds(0, NT - 1)], small_send.at[4])


def finish(packed_ref, sigma_ref, residual_ref, norms_ref):
    sigma_ref[...] = packed_ref[0:K]
    residual_ref[...] = packed_ref[K : 2 * K]
    norms_ref[...] = packed_ref[2 * K : 2 * K + 1, 0:K]


def shards(trial_vectors, couplings, neighbours, live_slots, energies):
    hbm = pl.BlockSpec(memory_space=pltpu.HBM)
    vmem = pl.BlockSpec(memory_space=pltpu.VMEM)
    dma = pltpu.SemaphoreType.DMA
    packed = pl.pallas_call(
        kernel,
        out_shape=pltpu.VMEM((3 * K, S), F32),
        in_specs=[hbm] * 5,
        out_specs=vmem,
        scratch_shapes=[
            pltpu.VMEM((K, S), F32),
            pltpu.VMEM((1, S), F32),
            pltpu.VMEM((NS, S, S), F32),
            pltpu.VMEM((NS, S, 2 * S), BF16),
            pltpu.SMEM((1, NS), jnp.int32),
            pltpu.SMEM((1, NS), jnp.int32),
            pltpu.VMEM((64, K, S), F32),
            pltpu.VMEM((NS, K, S), F32),
            pltpu.VMEM((NS, K, S), F32),
            pltpu.VMEM((8, S), F32),
            pltpu.VMEM((8, S), F32),
            pltpu.VMEM((8, S), F32),
            pltpu.VMEM((8, S), F32),
            pltpu.VMEM((8, S), F32),
            pltpu.VMEM((NT, S), F32),
            pltpu.VMEM((NS, S), F32),
            pltpu.VMEM((NT, S), F32),
            pltpu.VMEM((NS, S), F32),
            pltpu.VMEM((NT, S), F32),
            dma((4,)),
            dma((NS // CHUNK,)),
            dma((1,)),
            dma((NZ,)),
            dma((1,)),
            dma((1,)),
            dma((1,)),
            dma((1,)),
            dma((5,)),
            dma((5,)),
        ],
        compiler_params=pltpu.CompilerParams(collective_id=0, has_side_effects=True),
        name="davidson",
    )(
        trial_vectors.reshape(K, S),
        couplings.reshape(NS, S, S),
        neighbours.reshape(1, NS),
        live_slots.reshape(1, NS),
        energies,
    )
    sigma, residual, norms = pl.pallas_call(
        finish,
        out_shape=(
            jax.ShapeDtypeStruct((K, S), F32),
            jax.ShapeDtypeStruct((K, S), F32),
            jax.ShapeDtypeStruct((1, K), F32),
        ),
        in_specs=[vmem],
        out_specs=(vmem, vmem, vmem),
        name="finish",
    )(pltpu.with_memory_space_constraint(packed, pltpu.VMEM))
    return sigma.reshape(K, 1, S), residual.reshape(K, 1, S), norms.reshape(K)


def solution(mesh):
    return jax.shard_map(
        shards,
        mesh=mesh,
        in_specs=(
            P(None, ("tgt", "src"), None),
            P("tgt", "src", None, None),
            P("tgt", "src"),
            P("tgt", "src"),
            P(("tgt", "src"), None),
        ),
        out_specs=(P(None, ("tgt", "src"), None), P(None, ("tgt", "src"), None), P()),
        check_vma=False,
    )
```

```python
import functools

import jax
import jax.numpy as jnp
from jax import lax
from jax.experimental import pallas as pl
from jax.experimental.pallas import tpu as pltpu
from jax.sharding import PartitionSpec as P

MESH = pl.DeviceIdType.MESH
F32 = jnp.float32
BF16 = jnp.bfloat16
HIGHEST = lax.Precision.HIGHEST

NZ, NX, NT = 8, 4, 16
NS = NZ * NX
K, S = 8, 128
SHIFT = 2.0
CHUNK = 8
NT_DIMS = (((1,), (1,)), ((), ()))


def remote(src, dst, send_sem, recv_sem, device):
    return pltpu.make_async_remote_copy(
        src_ref=src,
        dst_ref=dst,
        send_sem=send_sem,
        recv_sem=recv_sem,
        device_id=device,
        device_id_type=MESH,
    )


def drain(ref, sem):
    pltpu.make_async_copy(ref, ref, sem).wait()


def far_first(n, count):
    return count // 2 + (1 - 2 * (n % 2)) * ((n + 1) // 2)


def as_row(pairs):
    full = jnp.concatenate([pairs, jnp.zeros_like(pairs)], axis=0)
    return lax.dot_general(
        jnp.ones((8, S), F32), full, NT_DIMS, precision=HIGHEST, preferred_element_type=F32
    )


def as_row8(tile):
    total = jnp.broadcast_to(jnp.sum(tile, axis=1, keepdims=True), (K, S))
    lane = lax.broadcasted_iota(jnp.int32, (K, S), 1)
    sub = lax.broadcasted_iota(jnp.int32, (K, S), 0)
    return jnp.sum(jnp.where(lane == sub, total, 0.0), axis=0, keepdims=True)


def as_tile(row):
    return pltpu.roll(jnp.broadcast_to(row, (K, S)), S - K * (K - 1), 1, stride=K, stride_axis=0)


def kernel(
    trial_hbm,
    couplings_hbm,
    neighbours_hbm,
    live_hbm,
    energies_hbm,
    packed_ref,
    own,
    energy,
    raw,
    halves,
    index,
    live,
    rows,
    parts,
    sums,
    row_p,
    row_g,
    row_q,
    row_s,
    row_u,
    tgt_p,
    plane_p,
    tgt_g,
    plane_s,
    tgt_s,
    load_sem,
    chunk_sem,
    z_send,
    z_recv,
    x_send,
    x_recv,
    part_send,
    part_recv,
    small_send,
    small_recv,
):
    t, s = lax.axis_index("tgt"), lax.axis_index("src")
    z, x = s // NX, s % NX

    loads = [
        pltpu.make_async_copy(trial_hbm, own, load_sem.at[0]),
        pltpu.make_async_copy(energies_hbm, energy, load_sem.at[1]),
        pltpu.make_async_copy(neighbours_hbm, index, load_sem.at[2]),
        pltpu.make_async_copy(live_hbm, live, load_sem.at[3]),
    ]
    loads[0].start()

    barrier = pltpu.get_barrier_semaphore()

    def greet(device):
        pl.semaphore_signal(barrier, inc=1, device_id=device, device_id_type=MESH)

    def along_z(d):
        return lax.rem(z + d, NZ) * NX + x

    def along_x(d):
        return z * NX + lax.rem(x + d, NX)

    def greet_beside(d, _):
        greet((lax.rem(t + 1, NT), along_x(d)))
        greet((lax.rem(t + NT - 1, NT), along_x(d)))

    lax.fori_loop(0, NZ - 1, lambda n, _: greet((t, along_z(far_first(n, NZ)))), None, unroll=True)
    lax.fori_loop(0, NT - 3, lambda n, _: greet((lax.rem(t + far_first(n, NT), NT), s)), None, unroll=True)
    lax.fori_loop(0, NX, greet_beside, None, unroll=True)
    lax.fori_loop(1, NX, lambda d, _: greet((t, along_x(d))), None, unroll=True)

    for load in loads[1:]:
        load.start()
    fetches = [
        pltpu.make_async_copy(
            couplings_hbm.at[pl.ds(c * CHUNK, CHUNK)], raw.at[pl.ds(c * CHUNK, CHUNK)], chunk_sem.at[c]
        )
        for c in range(NS // CHUNK)
    ]
    for fetch in fetches:
        fetch.start()
    loads[0].wait()
    pl.semaphore_wait(barrier, NZ - 1 + 2 * NX + NT - 3 + NX - 1)

    block = (t % 2) * NS
    mine = block + s

    def send_z(n, _):
        to = (t, along_z(far_first(n, NZ)))
        remote(own, rows.at[mine], z_send.at[0], z_recv.at[z], to).start()

    lax.fori_loop(0, NZ - 1, send_z, None, unroll=True)
    here = pltpu.make_async_copy(own, rows.at[mine], load_sem.at[0])
    here.start()

    def forward(src, j):
        at = block + j * NX + x
        beside = (t + NT - 1 + 2 * (j // 4)) % NT

        for n in range(NX):
            to = along_x(far_first(n, NX))
            for plane in (beside, t) if n < NX - 1 else (beside,):
                remote(src, rows.at[at], x_send.at[0], x_recv.at[0], (plane, to)).start()

    forward(own, z)

    def split(i, _):
        tile = raw[i]
        high = tile.astype(BF16)
        halves[i, :, 0:S] = high
        halves[i, :, S : 2 * S] = (tile - high.astype(F32)).astype(BF16)

    for c, fetch in enumerate(fetches):
        fetch.wait()
        lax.fori_loop(c * CHUNK, (c + 1) * CHUNK, split, None, unroll=2)
    for load in loads[1:]:
        load.wait()
    here.wait()

    for d in (1, 7, 2, 6, 3, 5, 4):
        j = (z + d) % NZ
        row = rows.at[block + j * NX + x]
        drain(row, z_recv.at[j])
        forward(row, j)
    drain(rows.at[pl.ds(0, 2 * NS - NZ)], x_recv.at[0])

    def target(n):
        to_z = lax.rem(z + far_first(n // NX, NZ), NZ)
        return to_z * NX + lax.rem(x + far_first(n % NX, NX), NX)

    def share(n, _):
        i = target(n)
        found = rows[lax.rem(index[0, i], 64)] * live[0, i].astype(F32)
        high = found.astype(BF16).astype(F32)
        low = found - high
        left = jnp.concatenate(
            [jnp.concatenate([high, low], 0), jnp.concatenate([high, jnp.zeros_like(high)], 0)], 1
        ).astype(BF16)
        both = lax.dot_general(left, halves[i], NT_DIMS, preferred_element_type=F32)
        parts[i] = both[0:K] + both[K : 2 * K]

    def send_part(n, _):
        to = target(n)
        remote(parts.at[to], sums.at[s], part_send.at[0], part_recv.at[0], (t, to)).start()

    for first, last in ((0, 4), (4, 12), (12, 20), (20, NS)):
        lax.fori_loop(first, last, share, None, unroll=True)
        lax.fori_loop(first, min(last, NS - 1), send_part, None, unroll=True)

    def outer(pairs, left, right):
        return tuple(
            pairs[l] + left * jnp.broadcast_to(right[l : l + 1], (K, S)) for l in range(K)
        )

    vector = own[...]
    diagonal = vector * (energy[...] - SHIFT)
    zeros = tuple(jnp.zeros((K, S), F32) for _ in range(K))
    pairs = lax.fori_loop(
        0, NS // 2, lambda i, p: outer(p, rows[block + i], parts[i]), zeros, unroll=8
    )
    pairs = lax.fori_loop(
        NS // 2, NS, lambda i, p: outer(p, rows[block + i], parts[i]), pairs, unroll=8
    )
    pairs = outer(pairs, vector, diagonal)
    row_p[...] = as_row(jnp.concatenate(pairs[::-1], 0))

    def send_tgt(src, buf, sem):
        def one(n, _):
            remote(
                src.at[pl.ds(0, 1)],
                buf.at[pl.ds(t, 1)],
                small_send.at[sem],
                small_recv.at[sem],
                (lax.rem(t + far_first(n, NT), NT), s),
            ).start()

        lax.fori_loop(0, NT - 1, one, None, unroll=True)
        buf[pl.ds(t, 1), :] = src[0:1, :]

    def wait_tgt(buf, sem):
        drain(buf.at[pl.ds(0, NT - 1)], small_recv.at[sem])
        return jnp.sum(buf[...], axis=0, keepdims=True)

    def send_plane(src, buf, sem):
        def one(n, _):
            to_z = lax.rem(z + far_first(n // NX, NZ), NZ)
            to_x = lax.rem(x + far_first(n % NX, NX), NX)
            remote(
                src.at[pl.ds(0, 1)],
                buf.at[pl.ds(s, 1)],
                small_send.at[sem],
                small_recv.at[sem],
                (t, to_z * NX + to_x),
            ).start()

        lax.fori_loop(0, NS - 1, one, None, unroll=True)
        buf[pl.ds(s, 1), :] = src[0:1, :]

    def wait_plane(buf, sem):
        drain(buf.at[pl.ds(0, NS - 1)], small_recv.at[sem])
        return jnp.sum(buf[...], axis=0, keepdims=True)

    send_tgt(row_p, tgt_p, 0)

    def gram(i, p):
        return outer(p, rows[block + i], rows[block + i])

    pairs = lax.fori_loop(0, NS, gram, zeros, unroll=8)
    row_g[...] = as_row(jnp.concatenate(pairs[::-1], 0))
    send_tgt(row_g, tgt_g, 1)

    drain(sums.at[pl.ds(0, NS - 1)], part_recv.at[0])
    sums[s] = parts[s]
    shifted = jnp.sum(sums[...], axis=0) + diagonal
    row_s[...] = jnp.broadcast_to(as_row8(shifted * shifted), (8, S))
    send_plane(row_s, plane_s, 3)
    packed_ref[2 * K : 3 * K] = jnp.zeros((K, S), F32)
    packed_ref[0:K] = shifted + SHIFT * vector

    row_q[...] = jnp.broadcast_to(wait_tgt(tgt_p, 0), (8, S))
    send_plane(row_q, plane_p, 2)

    metric = as_tile(wait_tgt(tgt_g, 1))
    lane = lax.broadcasted_iota(jnp.int32, (K, S), 1)
    sub = lax.broadcasted_iota(jnp.int32, (K, S), 0)
    norms2 = jnp.sum(jnp.where(lane == sub, metric, 0.0), axis=0, keepdims=True)
    work = metric
    solved = [vector, jnp.where(lane == sub, 1.0, 0.0)]
    factors = []
    for j in range(K):
        column = jnp.broadcast_to(work[:, j : j + 1], (K, S))
        pivot = lax.rsqrt(jnp.broadcast_to(column[j : j + 1], (K, S)))
        column = jnp.where(sub >= j, column * pivot, 0.0)
        factors.append((column, pivot))
        line = jnp.sum(jnp.where(lane == sub, column, 0.0), axis=0, keepdims=True)
        work = work - column * jnp.broadcast_to(line, (K, S))
        for n in range(2):
            top = jnp.broadcast_to(solved[n][j : j + 1], (K, S)) * pivot
            below = solved[n] - jnp.where(sub > j, column * top, 0.0)
            solved[n] = jnp.where(sub == j, top, below)
    for j in reversed(range(K)):
        column, pivot = factors[j]
        for n in range(2):
            dots = jnp.sum(jnp.where(sub > j, column * solved[n], 0.0), axis=0, keepdims=True)
            value = (solved[n] - jnp.broadcast_to(dots, (K, S))) * pivot
            solved[n] = jnp.where(sub == j, value, solved[n])
    solved, inverse = solved

    row_u[...] = jnp.broadcast_to(wait_plane(plane_s, 3), (8, S))
    send_tgt(row_u, tgt_s, 4)

    def times(left, right):
        total = jnp.zeros((K, S), F32)
        for j in range(K):
            total = total + jnp.broadcast_to(left[:, j : j + 1], (K, S)) * jnp.broadcast_to(
                right[j : j + 1], (K, S)
            )
        return total

    projected = as_tile(wait_plane(plane_p, 2))
    packed_ref[K : 2 * K] = shifted - times(projected, solved)
    square_mesh = (lane < K) & (sub < K)
    mixing = times(projected, inverse)
    missing = projected - times(mixing, metric)
    taken = as_row8(jnp.where(square_mesh, mixing * (projected + missing), 0.0))

    scale = 1.0 / jnp.where(lane[0:1] < K, norms2, 1.0)

    drain(rows.at[pl.ds(0, NZ - 1)], z_send.at[0])
    drain(rows.at[pl.ds(0, 2 * NS - NZ)], x_send.at[0])
    drain(parts.at[pl.ds(0, NS - 1)], part_send.at[0])
    for sem, buf, count in ((0, tgt_p, NT), (1, tgt_g, NT), (2, plane_p, NS), (3, plane_s, NS)):
        drain(buf.at[pl.ds(0, count - 1)], small_send.at[sem])

    left_over = jnp.maximum(wait_tgt(tgt_s, 4) - taken, 0.0)
    packed_ref[2 * K : 2 * K + 1] = jnp.sqrt(left_over * scale)
    drain(tgt_s.at[pl.ds(0, NT - 1)], small_send.at[4])


def finish(packed_ref, sigma_ref, residual_ref, norms_ref):
    sigma_ref[...] = packed_ref[0:K]
    residual_ref[...] = packed_ref[K : 2 * K]
    norms_ref[...] = packed_ref[2 * K : 2 * K + 1, 0:K]


def shards(trial_vectors, couplings, neighbours, live_slots, energies):
    hbm = pl.BlockSpec(memory_space=pltpu.HBM)
    vmem = pl.BlockSpec(memory_space=pltpu.VMEM)
    dma = pltpu.SemaphoreType.DMA
    packed = pl.pallas_call(
        kernel,
        out_shape=pltpu.VMEM((3 * K, S), F32),
        in_specs=[hbm] * 5,
        out_specs=vmem,
        scratch_shapes=[
            pltpu.VMEM((K, S), F32),
            pltpu.VMEM((1, S), F32),
            pltpu.VMEM((NS, S, S), F32),
            pltpu.VMEM((NS, S, 2 * S), BF16),
            pltpu.SMEM((1, NS), jnp.int32),
            pltpu.SMEM((1, NS), jnp.int32),
            pltpu.VMEM((64, K, S), F32),
            pltpu.VMEM((NS, K, S), F32),
            pltpu.VMEM((NS, K, S), F32),
            pltpu.VMEM((8, S), F32),
            pltpu.VMEM((8, S), F32),
            pltpu.VMEM((8, S), F32),
            pltpu.VMEM((8, S), F32),
            pltpu.VMEM((8, S), F32),
            pltpu.VMEM((NT, S), F32),
            pltpu.VMEM((NS, S), F32),
            pltpu.VMEM((NT, S), F32),
            pltpu.VMEM((NS, S), F32),
            pltpu.VMEM((NT, S), F32),
            dma((4,)),
            dma((NS // CHUNK,)),
            dma((1,)),
            dma((NZ,)),
            dma((1,)),
            dma((1,)),
            dma((1,)),
            dma((1,)),
            dma((5,)),
            dma((5,)),
        ],
        compiler_params=pltpu.CompilerParams(collective_id=0, has_side_effects=True),
        name="davidson",
    )(
        trial_vectors.reshape(K, S),
        couplings.reshape(NS, S, S),
        neighbours.reshape(1, NS),
        live_slots.reshape(1, NS),
        energies,
    )
    sigma, residual, norms = pl.pallas_call(
        finish,
        out_shape=(
            jax.ShapeDtypeStruct((K, S), F32),
            jax.ShapeDtypeStruct((K, S), F32),
            jax.ShapeDtypeStruct((1, K), F32),
        ),
        in_specs=[vmem],
        out_specs=(vmem, vmem, vmem),
        name="finish",
    )(pltpu.with_memory_space_constraint(packed, pltpu.VMEM))
    return sigma.reshape(K, 1, S), residual.reshape(K, 1, S), norms.reshape(K)


def solution(mesh):
    return jax.shard_map(
        shards,
        mesh=mesh,
        in_specs=(
            P(None, ("tgt", "src"), None),
            P("tgt", "src", None, None),
            P("tgt", "src"),
            P("tgt", "src"),
            P(("tgt", "src"), None),
        ),
        out_specs=(P(None, ("tgt", "src"), None), P(None, ("tgt", "src"), None), P()),
        check_vma=False,
    )
```
